512 devices in a mesh: tp: 16 (over z_lo, core), lat: 32 (over y, x, z_hi).
Axes of the slice: x: 4, y: 4, z: 16 (z_hi: 2, z_lo: 8; z = z_hi * 8 + z_lo), core: 2. Of those that a mesh axis runs over, the one named last changes fastest.
Arguments:
- resid: bfloat16 [256, 8192], P(None, 'tp'), may hold values from -6 to 6
- gain: float32 [8192], P('tp'), may hold values from 0.2 to 2.5
- w_gate: bfloat16 [8192, 28672], P('tp', 'lat'), may hold values from -0.0625 to 0.0625
- w_up: bfloat16 [8192, 28672], P('tp', 'lat'), may hold values from -0.0625 to 0.0625
- w_down: bfloat16 [28672, 8192], P('lat', 'tp'), may hold values from -0.0625 to 0.0625
- cotangent: bfloat16 [256, 8192], P(None, 'tp'), may hold values from -6 to 6
- enc_tiles: bfloat16 [160, 8192, 128], P('lat', 'tp'), may hold values from -0.0625 to 0.0625
- enc_bias: float32 [160, 128], P('lat'), may hold values from -3 to 3
- dec_tiles: bfloat16 [160, 128, 8192], P('lat', None, 'tp'), may hold values from -0.0625 to 0.0625
- tile_blocks: int32 [160], P('lat'), may hold values from 0 to 8192, as said below
- owner_counts: int32 [32], P('lat'), may hold values from 1 to 5, as said below
- token_blocks: int32 [256, 64], replicated, may hold values from 0 to 8192, as said below
Outputs:
- resid_grad: bfloat16 [256, 8192], P(None, 'tp')
- attribution: float32 [256, 160, 128], P('tp', 'lat')
The draws below stay inside these ranges and needn't reach their ends.
Inputs may be any that keep to these rules, and one draw needn't show every extreme that they name: `tile_blocks`: owner o holds tile slots o * 5 to o * 5 + 4; its first owner_counts[o] slots hold distinct block ids below 8192, the other slots hold 8192. `owner_counts`: some owner uses all 5 slots. `token_blocks`: 8192 marks an empty slot; an id may stand more than once in one token's list.
All inputs are finite; a program needn't handle non-finite values.
Results may differ from the reference program's by a relative error of at most 0.0054.
Values may be sent and summed in bfloat16 or wider, within the bound.
A program may use at most 64 MiB of HBM per device.

```python
import jax
import jax.numpy as jnp
from jax import lax

D = 8192
FF = 28672
TOK = 256
LAT = 128
NBLK = 8192
S = 64
CAP = 5
TILES = 160
N_LAT = 32


def feature_ramp(key, low, high):
    position = jnp.arange(D, dtype=jnp.float32) / max(D - 1, 1)
    ramp = low * (high / low) ** position
    rough = jnp.exp(jax.random.uniform(key, (D,), jnp.float32, jnp.log(0.8), jnp.log(1.25)))
    return ramp * rough


def draw_gain(key, part):
    base = jax.random.fold_in(key, 31)
    values = feature_ramp(base, 0.4, 1.4)
    return jnp.clip(values, 0.2, 2.5).astype(jnp.float32)


def draw_resid(key, part):
    base = jax.random.fold_in(key, 37)
    scales = feature_ramp(jax.random.fold_in(base, 1), 0.5, 1.5)
    noise = jax.random.normal(jax.random.fold_in(base, 2), (TOK, D), jnp.float32)
    return jnp.clip(noise * scales[None, :], -6.0, 6.0).astype(jnp.bfloat16)


def tile_layout(key):
    base = jax.random.fold_in(key, 7)
    counts = jax.random.randint(jax.random.fold_in(base, 1), (N_LAT,), 1, CAP + 1)
    fullest = jax.random.randint(jax.random.fold_in(base, 2), (), 0, N_LAT)
    counts = jnp.where(jnp.arange(N_LAT) == fullest, CAP, counts).astype(jnp.int32)
    chosen = jax.random.permutation(jax.random.fold_in(base, 3), NBLK)[:TILES].astype(jnp.int32)
    slot_ids = jnp.arange(TILES)
    used = slot_ids % CAP < counts[slot_ids // CAP]
    tiles = jnp.where(used, chosen, NBLK).astype(jnp.int32)
    return (counts, tiles, chosen)


def draw_owner_counts(key, part):
    return tile_layout(key)[0]


def draw_tile_blocks(key, part):
    return tile_layout(key)[1]


def draw_token_blocks(key, part):
    counts, tiles, chosen = tile_layout(key)
    base = jax.random.fold_in(key, 11)
    owner = jax.random.randint(jax.random.fold_in(base, 1), (TOK, S), 0, N_LAT)
    within = jax.random.randint(jax.random.fold_in(base, 2), (TOK, S), 0, CAP) % counts[owner]
    live_id = chosen[owner * CAP + within]
    other = jax.random.randint(jax.random.fold_in(base, 3), (TOK, S), 0, NBLK)
    kind = jax.random.randint(jax.random.fold_in(base, 4), (TOK, S), 0, 4)
    result = jnp.where(kind < 2, live_id, jnp.where(kind == 2, other, NBLK))
    return result.astype(jnp.int32)


def with_spikes(array, key, source, target, shards_of, factor):
    owner, partner = [(jnp.arange(array.shape[dim]) // (array.shape[dim] // shards_of)).reshape([-1 if axis == dim else 1 for axis in range(array.ndim)]) for dim in (source, target)]
    chosen = jax.random.permutation(key, shards_of)[partner]
    strong = (owner == chosen) | (owner == (partner + shards_of // 2) % shards_of)
    return jnp.where(strong, factor * array, array)


def steps_of(rng, dims, pieces, smallest, largest):
    factor_of = 1.0
    for axis_at, blocks in pieces:
        draws = jax.random.uniform(jax.random.fold_in(jax.random.fold_in(rng, 6), axis_at), (blocks,), jnp.float32, smallest / len(pieces), largest / len(pieces))
        factor_of = factor_of * jnp.repeat(jnp.exp(draws), dims[axis_at] // blocks).reshape((-1,) + (1,) * (len(dims) - 1 - axis_at))
    return factor_of


def centred(stream_key, dims, spread, most, pieces=(), kind=jnp.bfloat16):
    entries = jax.random.normal(stream_key, dims, jnp.float32) * spread
    if len(pieces) > 0:
        entries = steps_of(stream_key, dims, pieces, -0.22, 0.18) * entries
    return jnp.clip(entries, min=-most, max=most).astype(kind)


def gaussian_with(key, extent, spread, bound, split, heavy, held_as=jnp.bfloat16):
    array = spread * jax.random.normal(key, extent, jnp.float32)
    if split:
        array = array * steps_of(key, extent, split, -0.22, 0.18)
    return jnp.clip(with_spikes(array, jax.random.fold_in(key, 3), *heavy), -bound, bound).astype(held_as)


def setup_inputs(seed: int = 0) -> dict:
    splits = jax.random.split(jax.random.key(seed), 13)
    resid = draw_resid(jax.random.fold_in(splits[12], 71), 0)
    gain = draw_gain(jax.random.fold_in(splits[12], 71), 0)
    w_gate = centred(splits[2], (D, FF), D ** -0.5, 0.0625, ((0, 16), (1, 32)))
    w_up = centred(splits[3], (D, FF), D ** -0.5, 0.0625, ((0, 16), (1, 32)))
    w_down = gaussian_with(splits[4], (FF, D), FF ** -0.5, 0.0625, ((0, 32), (1, 16)), (0, 1, 32, 2.75))
    cotangent = centred(splits[5], (TOK, D), 1.0, 6.0, ((1, 16),))
    enc_tiles = centred(splits[6], (TILES, D, LAT), D ** -0.5, 0.0625, ((0, 32), (1, 16)))
    enc_bias = centred(splits[7], (TILES, LAT), 0.5, 3.0, ((0, 32),), jnp.float32)
    dec_tiles = centred(splits[8], (TILES, LAT, D), D ** -0.5, 0.0625, ((0, 32), (2, 16)))
    tile_blocks = draw_tile_blocks(jax.random.fold_in(splits[12], 71), 0)
    owner_counts = draw_owner_counts(jax.random.fold_in(splits[12], 71), 0)
    token_blocks = draw_token_blocks(jax.random.fold_in(splits[12], 71), 0)
    return {"resid": resid, "gain": gain, "w_gate": w_gate, "w_up": w_up, "w_down": w_down, "cotangent": cotangent, "enc_tiles": enc_tiles, "enc_bias": enc_bias, "dec_tiles": dec_tiles, "tile_blocks": tile_blocks, "owner_counts": owner_counts, "token_blocks": token_blocks}


def reference(resid, gain, w_gate, w_up, w_down, cotangent, enc_tiles, enc_bias, dec_tiles, tile_blocks, owner_counts, token_blocks):
    resid_f = resid.astype(jnp.float32)
    rinv = lax.rsqrt(lax.optimization_barrier(jnp.sum(resid_f * resid_f, axis=1)) / D + 1e-05)
    scaled = (resid_f * gain).astype(jnp.bfloat16)
    gate = rinv[:, None] * jnp.dot(scaled, w_gate, preferred_element_type=jnp.float32)
    up = rinv[:, None] * jnp.dot(scaled, w_up, preferred_element_type=jnp.float32)
    hgrad = jnp.dot(cotangent, w_down.T, preferred_element_type=jnp.float32)
    sig = jax.nn.sigmoid(gate)
    d_gate = (hgrad * up * sig * (1.0 + gate * (1.0 - sig))).astype(jnp.bfloat16)
    d_up = (hgrad * gate * sig).astype(jnp.bfloat16)
    feat = jnp.dot(d_gate, w_gate.T, preferred_element_type=jnp.float32) + jnp.dot(d_up, w_up.T, preferred_element_type=jnp.float32)
    norm_term = lax.optimization_barrier(jnp.sum(resid_f * gain * feat, axis=1))
    resid_grad = (cotangent.astype(jnp.float32) + rinv[:, None] * gain * feat - resid_f * (rinv ** 3 * norm_term / D)[:, None]).astype(jnp.bfloat16)
    pre = jnp.einsum('td,jdl->tjl', resid.astype(jnp.float32), enc_tiles.astype(jnp.float32))
    grad = jnp.einsum('td,jld->tjl', resid_grad.astype(jnp.float32), dec_tiles.astype(jnp.float32))
    slot_ids = jnp.arange(TILES, dtype=jnp.int32)
    used = slot_ids % CAP < owner_counts[slot_ids // CAP]
    match = jnp.any(token_blocks[:, :, None] == tile_blocks[None, None, :], axis=1)
    live = jnp.logical_and(match, used[None, :]).astype(jnp.float32)
    attribution = -jnp.maximum(pre + enc_bias[None], 0.0) * live[:, :, None] * grad
    return (resid_grad, attribution)
```

```python
import jax
import jax.numpy as jnp
from jax import lax
from jax.experimental import pallas as pl
from jax.experimental.pallas import tpu as pltpu
from jax.sharding import PartitionSpec as P

BF = jnp.bfloat16
F32 = jnp.float32
WIDTH = 8192
TOK = 256
G = 7
NR = 2
RT, CT = 256 // NR, 128 // NR
HT = CT // 2
NS = G * NR
PART = NS // 2
FINISH = 3 * NR // 2
GATHER = 5 * NR
SKIP = NS - 3 * NR // 2
STEPS = 2 * NS + 2
VMEM = pl.BlockSpec(memory_space=pltpu.VMEM)
SMEM = pl.BlockSpec(memory_space=pltpu.SMEM)
HBM = pl.BlockSpec(memory_space=pltpu.HBM)


def dot(a, b):
    return jnp.dot(a, b, preferred_element_type=F32)


def dot_t(a, b, precision=None):
    return lax.dot_general(
        a, b, (((1,), (1,)), ((), ())), precision=precision, preferred_element_type=F32
    )


def row_sums(x):
    folded = x[:, 0:128]
    for k in range(1, x.shape[1] // 128):
        folded = folded + x[:, 128 * k : 128 * (k + 1)]
    return dot_t(jnp.ones((8, 128), F32), folded, lax.Precision.HIGHEST)


def as_column(row, n):
    full = jnp.broadcast_to(row, (n, n))
    same = lax.broadcasted_iota(jnp.int32, (n, n), 0) == lax.broadcasted_iota(jnp.int32, (n, n), 1)
    return jnp.sum(jnp.where(same, full, 0.0), axis=1, keepdims=True)


def copy(src, dst, send_sem, recv_sem, **device):
    return pltpu.make_async_remote_copy(
        src_ref=src,
        dst_ref=dst,
        send_sem=send_sem,
        recv_sem=recv_sem,
        device_id=device,
        device_id_type=pl.DeviceIdType.MESH,
    )


def loop(n, body, start=0):
    def step(i, carry):
        body(i)
        return carry

    lax.fori_loop(start, n, step, 0)


def kernel(
    resid_h,
    gain_h,
    w_gate_h,
    w_up_h,
    w_down_h,
    cot_h,
    enc_h,
    bias_h,
    dec_h,
    tile_blocks_h,
    owner_counts,
    tokens_h,
    rg_out,
    att_out,
    resid,
    gain,
    w_gate,
    w_up,
    w_down,
    cot,
    enc,
    bias,
    dec,
    tile_blocks,
    tokens,
    part,
    scaled,
    psend,
    precv,
    rs_recv,
    rs_send,
    x_recv,
    d_all,
    acc,
    rinv_s,
    sq_own,
    sq_recv,
    fsend,
    frecv,
    hsend,
    hrecv,
    n_own,
    n_recv,
    rg_own,
    rg_all,
    terms,
    tp_send,
    tp_recv,
    tz_send,
    tz_recv,
    gate_term,
    psem,
    precvsem,
    rssem,
    rsrecv,
    xsem,
    agsend,
    agrecv,
    agother,
    sqsem,
    fsem,
    hsem,
    nsem,
    rgsem,
    tpsem,
    tzsem,
    insem,
):
    t, l = lax.axis_index("tp"), lax.axis_index("lat")
    z, c = lax.div(t, 2), lax.rem(t, 2)
    p, h = lax.div(l, 2), lax.rem(l, 2)
    y, x = lax.div(p, 4), lax.rem(p, 4)
    other = t + 1 - 2 * c
    right = lax.div(z, 4)
    step_in = 1 - 2 * right
    q = z + right * (7 - 2 * z)
    inward = t + 2 * step_in
    outward = t - 2 * step_in
    middle = lax.div(q, 3)
    beside = lax.div(q, 2) - middle
    lag = NS + (GATHER - NS) * beside + (FINISH + 1 - NS) * middle
    mate = l + 1 - 2 * h
    u = h * 16 + t

    ahead = 2 + (NS - 2) // 3 * q
    early = lax.div(q + 2, 3)
    flag = lag + 1 + early
    group = 8 * lax.rem(x + y, 2) + lax.div(p, 2)

    def owner_of(g):
        e = lax.rem(g, 8)
        return 2 * e + lax.rem(lax.div(g, 8) + lax.div(e, 2), 2)

    def group_of(pp):
        return 8 * lax.rem(lax.rem(pp, 4) + lax.div(pp, 4), 2) + lax.div(pp, 2)

    def peer_xy(j):
        return lax.rem(y + lax.div(j, 4), 4) * 4 + lax.rem(x + lax.rem(j, 4), 4)

    def peer_tp(j):
        return lax.rem(t + j, 16)

    def peer_z(j):
        return lax.rem(z + j, 8)

    loads = [
        pltpu.make_async_copy(src, dst, insem.at[k])
        for k, (src, dst) in enumerate(
            (
                (resid_h, resid),
                (gain_h, gain),
                (w_gate_h.at[:, 0:256], w_gate.at[:, 0:256]),
                (w_up_h.at[:, 0:256], w_up.at[:, 0:256]),
                (cot_h, cot),
                (w_down_h.at[0:256], w_down.at[0:256]),
                (w_gate_h.at[:, 256:896], w_gate.at[:, 256:896]),
                (w_up_h.at[:, 256:896], w_up.at[:, 256:896]),
                (w_down_h.at[256:896], w_down.at[256:896]),
                (enc_h, enc),
                (tokens_h, tokens),
                (dec_h, dec),
                (bias_h, bias),
                (tile_blocks_h, tile_blocks),
            )
        )
    ]
    for load in loads[:9]:
        load.start()

    barrier = pltpu.get_barrier_semaphore()

    def greet(**device):
        pl.semaphore_signal(
            barrier, inc=1, device_id=device, device_id_type=pl.DeviceIdType.MESH
        )

    loop(16, lambda j: greet(tp=j, lat=mate))
    loop(16, lambda j: greet(tp=peer_tp(j), lat=l), 1)
    loop(16, lambda j: greet(tp=t, lat=peer_xy(j) * 2 + h), 1)

    loads[0].wait()
    loads[1].wait()
    resid_f = resid[...].astype(F32)
    scaled[...] = (resid_f * gain[...]).astype(BF)
    sq_own[...] = row_sums(resid_f * resid_f)[0:1]
    sq_recv[pl.ds(t, 1)] = sq_own[...][None]

    def products(n):
        g = lax.rem(n, G)
        lanes = pl.ds(pl.multiple_of(g * 128, 128), 128)
        rows = pl.ds(pl.multiple_of(lax.div(n, G) * RT, RT), RT)
        part[n, :, 0:128] = dot(scaled[rows, :], w_gate[:, lanes])
        part[n, :, 128:256] = dot(scaled[rows, :], w_up[:, lanes])
        part[n, :, 256:384] = dot_t(cot[rows, :], w_down[lanes, :])
        psend[n] = part[n, pl.ds(pl.multiple_of((1 - c) * CT, CT), CT), :].astype(BF)

    def to_partner(g):
        return copy(psend.at[g], precv.at[g], psem, precvsem.at[g], tp=other)

    for load in loads[2:6]:
        load.wait()
    products(0)

    @pl.when(q == 0)
    def _():
        rs_recv[...] = jnp.zeros_like(rs_recv)

    for load in loads[9:]:
        load.start()

    pl.semaphore_wait(barrier, 46)

    to_partner(0).start()

    def all_of(ref, send_sem, recv_sem):
        return copy(ref, ref, send_sem, recv_sem, tp=other)

    def squares_to(j):
        return copy(sq_own, sq_recv.at[t], sqsem.at[0], sqsem.at[1], tp=peer_tp(j))

    squares = all_of(sq_recv.at[0:15], sqsem.at[0], sqsem.at[1])

    loop(16, lambda j: squares_to(j).start(), 1)

    def first(g):
        products(g)
        to_partner(g).start()

    for load in loads[6:9]:
        load.wait()
    loop(ahead, first, 1)
    acc[...] = jnp.zeros_like(acc)

    def in_rs(k, g):
        return copy(rs_send.at[g, k], rs_recv.at[g, k], rssem, rsrecv.at[k, g], tp=inward)

    def across(k, g):
        return copy(rs_send.at[g, k], x_recv.at[g, k], rssem, xsem.at[k, g], tp=inward)

    def half_rows(k):
        return pl.ds(pl.multiple_of(c * CT + k * HT, HT), HT)

    def scatter_step(g):
        to_partner(g).wait_recv()
        for k in range(2):

            @pl.when(q > 0)
            def _():
                in_rs(k, g).wait_recv()

            value = part[g, half_rows(k), :] + precv[g, k * HT : (k + 1) * HT, :].astype(F32)
            value = value + rs_recv[g, k].astype(F32)
            rs_send[g, k] = value.astype(BF)

            @pl.when(q < 3)
            def _():
                in_rs(k, g).start()

            @pl.when(q == 3)
            def _():
                across(k, g).start()
                part[g, half_rows(k), :] = value

    def ag(where, k, g, **device):
        at = d_all.at[g, c, k]
        return copy(at, at, agsend.at[where], agrecv.at[k, g], **device)

    def to_other(g):
        at = d_all.at[g, c]
        return copy(at, at, agsend.at[2], agother.at[g], tp=other)

    def finish_step(g):
        for k in range(2):
            across(k, g).wait_recv()
            value = part[g, half_rows(k), :] + x_recv[g, k].astype(F32)
            first_row = lax.div(g, G) * RT + c * CT + k * HT
            scale = rinv_s[pl.ds(pl.multiple_of(first_row, HT), HT), :]
            gate, up = scale * value[:, 0:128], scale * value[:, 128:256]
            hgrad = value[:, 256:384]
            sig = jax.nn.sigmoid(gate)
            d_all[g, c, k, :, 0:128] = (
                hgrad * up * sig * (1.0 + gate * (1.0 - sig))
            ).astype(BF)
            d_all[g, c, k, :, 128:256] = (hgrad * gate * sig).astype(BF)
            ag(0, k, g, tp=outward).start()

            @pl.when(g >= SKIP)
            def _():
                ag(1, k, g, tp=outward - 2 * step_in).start()

        to_other(g).start()

    def passes(g):
        return (q > 0) & ((q != 2) | (g < SKIP))

    def gather_step(g):
        for k in range(2):
            ag(0, k, g, tp=outward).wait_recv()

            @pl.when(passes(g))
            def _():
                ag(0, k, g, tp=outward).start()

        to_other(g).start()

    def feature_step(n):
        to_other(n).wait_recv()
        g = lax.rem(n, G)
        lanes = pl.ds(pl.multiple_of(g * 128, 128), 128)
        rows = pl.ds(pl.multiple_of(lax.div(n, G) * RT, RT), RT)
        d = d_all[n].reshape(RT, 256)
        acc[rows, :] += dot_t(d[:, 0:128], w_gate[:, lanes]) + dot_t(d[:, 128:256], w_up[:, lanes])

    def feat_to(k, into):
        return copy(fsend.at[k], frecv.at[p], fsem.at[0], fsem.at[1], lat=into * 2 + h)

    feats = all_of(frecv.at[0:15], fsem.at[0], fsem.at[1])

    def feat_start(half):
        k0 = half * 8
        rows = pl.ds(pl.multiple_of(half * 128, 128), 128)
        fsend[pl.ds(k0, 8)] = acc[rows, :].astype(BF).reshape(8, 16, 512)

        def send(e):
            k = k0 + lax.rem(lax.div(p, 2) + e, 8)
            into = owner_of(k)

            @pl.when(into != p)
            def _():
                feat_to(k, into).start()

        loop(8, send)

    def inverse_norms():
        squares.wait_recv()
        total = sq_recv[0]
        for k in range(1, 16):
            total = total + sq_recv[k]
        column = as_column(lax.rsqrt(total / WIDTH + 1e-05), TOK)
        rinv_s[...] = jnp.broadcast_to(column, (TOK, 128))

    def tiles_to_partner(kind):
        return copy(
            tp_send.at[kind], tp_recv.at[kind], tpsem.at[0, kind], tpsem.at[1, kind], tp=other
        )

    def tiles_to(kind, j):
        zz = peer_z(j)
        return copy(
            tz_send.at[kind, zz],
            tz_recv.at[kind, z],
            tzsem.at[kind, 0],
            tzsem.at[kind, 1],
            tp=2 * zz + c,
        )

    def tiles_all(kind):
        return all_of(tz_recv.at[kind, 0:7], tzsem.at[kind, 0], tzsem.at[kind, 1])

    def tiles_start(kind):
        tp_send[kind] = terms[kind, :, 1 - c].astype(BF)
        tiles_to_partner(kind).start()

    def tiles_spread(kind):
        tiles_to_partner(kind).wait_recv()
        chip = terms[kind, :, c] + tp_recv[kind].astype(F32)
        terms[kind, :, c] = chip
        tz_send[kind] = chip.astype(BF)
        tz_recv[kind, z] = jnp.zeros((16, 640), BF)
        loop(8, lambda j: tiles_to(kind, j).start(), 1)

    def tiles_total(kind):
        tiles_all(kind).wait_recv()
        total = terms[kind, z, c]
        for k in range(8):
            total = total + tz_recv[kind, k].astype(F32)
        return total

    def pre_products():
        for load in loads[9:]:
            load.wait()
        for j in range(5):
            terms[0, :, :, :, 128 * j : 128 * (j + 1)] = dot(resid[...], enc[j]).reshape(
                8, 2, 16, 128
            )
        tiles_start(0)

    def step(s):
        @pl.when(s == NS * (1 - early))
        def _():
            pre_products()

        @pl.when(s < NS)
        def _():
            scatter_step(s)

        @pl.when(s + ahead < NS)
        def _():
            first(s + ahead)

        @pl.when(s == NS + (FINISH - NS) * early)
        def _():
            inverse_norms()

        @pl.when((q == 3) & (s >= FINISH) & (s < FINISH + NS))
        def _():
            finish_step(s - FINISH)

        @pl.when((s >= flag) & (s < flag + NS))
        def _():
            feature_step(s - flag)

            @pl.when(lax.rem(s - flag + 1, PART) == 0)
            def _():
                feat_start(lax.div(s - flag + 1, PART) - 1)

        @pl.when((q < 3) & (s >= lag) & (s < lag + NS))
        def _():
            gather_step(s - lag)

    loop(STEPS, step)

    frecv[p] = jnp.zeros((16, 512), BF)
    feats.wait_recv()
    own_rows = pl.ds(pl.multiple_of(group * 16, 16), 16)
    total = acc[own_rows, :]
    for k in range(16):
        total = total + frecv[k].astype(F32)
    hsend[...] = total.astype(BF)

    def to_mate():
        return copy(hsend, hrecv, hsem.at[0], hsem.at[1], lat=mate)

    to_mate().start()
    half = hsend[...].astype(F32)
    own_resid = resid[own_rows, :].astype(F32)
    n_own[...] = jnp.zeros_like(n_own)
    n_own[0:1, 0:16] = row_sums(own_resid * gain[...] * half)[0:1]
    n_recv[pl.ds(u, 1)] = n_own[...][None]

    def norm_to(j, half):
        return copy(
            n_own, n_recv.at[u], nsem.at[0], nsem.at[1], tp=peer_tp(j), lat=half
        )

    norms = all_of(n_recv.at[0:31], nsem.at[0], nsem.at[1])
    loop(16, lambda j: norm_to(j, mate).start())
    loop(16, lambda j: norm_to(j, l).start(), 1)

    lists = tokens[...]
    own_token = lax.broadcasted_iota(jnp.int32, (16, TOK), 0) + t * 16
    own_token = own_token == lax.broadcasted_iota(jnp.int32, (16, TOK), 1)
    for j in range(5):
        hits = jnp.max((lists == tile_blocks[j]).astype(F32), axis=0, keepdims=True)
        hits = jnp.broadcast_to(hits, (16, TOK))
        hit = jnp.sum(jnp.where(own_token, hits, 0.0), axis=1, keepdims=True)
        live = hit * jnp.where(owner_counts[0] > j, 1.0, 0.0)
        gate_term[:, 128 * j : 128 * (j + 1)] = jnp.broadcast_to(live, (16, 128))

    norms.wait_recv()
    norm = n_recv[0]
    for k in range(1, 32):
        norm = norm + n_recv[k]
    norm = as_column(norm[:, 0:16], 16)
    to_mate().wait_recv()
    feat = half + hrecv[...].astype(F32)
    rinv = rinv_s[own_rows, 0:1]
    rg_own[...] = (
        cot[own_rows, :].astype(F32)
        + rinv * gain[...] * feat
        - own_resid * (rinv * rinv * rinv * norm / WIDTH)
    ).astype(BF)

    def grad_to(j):
        pp = peer_xy(j)
        return copy(rg_own, rg_all.at[group], rgsem.at[0], rgsem.at[1], lat=pp * 2 + h)

    spread = all_of(rg_all.at[0:15], rgsem.at[0], rgsem.at[1])
    loop(16, lambda j: grad_to(j).start(), 1)
    tiles_spread(0)
    rg_all[group] = rg_own[...]
    spread.wait_recv()
    grads = rg_all[...].reshape(TOK, 512)
    for j in range(5):
        terms[1, :, :, :, 128 * j : 128 * (j + 1)] = dot_t(grads, dec[j]).reshape(8, 2, 16, 128)
    tiles_start(1)
    rg_out[...] = grads
    tiles_spread(1)
    pre = tiles_total(0)
    for j in range(5):
        lanes = slice(128 * j, 128 * (j + 1))
        gate_term[:, lanes] *= -jnp.maximum(pre[:, lanes] + bias[j : j + 1, :], 0.0)

    all_of(psend, psem, precvsem.at[0]).wait_send()
    all_of(rs_send, rssem, rsrecv.at[0, 0]).wait_send()

    def blocks_sent(where, n):
        all_of(d_all.at[0:n, 0], agsend.at[where], agrecv.at[0, 0]).wait_send()

    @pl.when(lax.rem(q, 2) == 1)
    def _():
        blocks_sent(0, NS)

    @pl.when(q == 2)
    def _():
        blocks_sent(0, SKIP)

    @pl.when(q == 3)
    def _():
        blocks_sent(1, NS - SKIP)

    blocks_sent(2, NS)
    squares.wait_send()
    feats.wait_send()
    spread.wait_send()
    to_mate().wait_send()
    norms.wait_send()
    for kind in range(2):
        tiles_to_partner(kind).wait_send()
    tiles_all(0).wait_send()

    grad = tiles_total(1)
    for j in range(5):
        lanes = slice(128 * j, 128 * (j + 1))
        att_out[j] = gate_term[:, lanes] * grad[:, lanes]

    tiles_all(1).wait_send()


def in_hbm(x):
    return pltpu.with_memory_space_constraint(x, pltpu.HBM)


def on_device(
    resid,
    gain,
    w_gate,
    w_up,
    w_down,
    cotangent,
    enc_tiles,
    enc_bias,
    dec_tiles,
    tile_blocks,
    owner_counts,
    token_blocks,
):
    dma = pltpu.SemaphoreType.DMA
    vmem = pltpu.VMEM
    resid_grad, attribution = pl.pallas_call(
        kernel,
        out_shape=(
            jax.ShapeDtypeStruct((TOK, 512), BF),
            jax.ShapeDtypeStruct((5, 16, 128), F32),
        ),
        in_specs=[HBM] * 10 + [SMEM, HBM],
        out_specs=(VMEM, VMEM),
        scratch_shapes=[
            vmem((TOK, 512), BF),
            vmem((1, 512), F32),
            vmem((512, 896), BF),
            vmem((512, 896), BF),
            vmem((896, 512), BF),
            vmem((TOK, 512), BF),
            vmem((5, 512, 128), BF),
            vmem((5, 128), F32),
            vmem((5, 128, 512), BF),
            pltpu.SMEM((5,), jnp.int32),
            vmem((64, TOK), jnp.int32),
            vmem((NS, RT, 384), F32),
            vmem((TOK, 512), BF),
            vmem((NS, CT, 384), BF),
            vmem((NS, CT, 384), BF),
            vmem((NS, 2, HT, 384), BF),
            vmem((NS, 2, HT, 384), BF),
            vmem((NS, 2, HT, 384), BF),
            vmem((NS, 2, 2, HT, 256), BF),
            vmem((TOK, 512), F32),
            vmem((TOK, 128), F32),
            vmem((1, TOK), F32),
            vmem((16, 1, TOK), F32),
            vmem((16, 16, 512), BF),
            vmem((16, 16, 512), BF),
            vmem((16, 512), BF),
            vmem((16, 512), BF),
            vmem((1, 128), F32),
            vmem((32, 1, 128), F32),
            vmem((16, 512), BF),
            vmem((16, 16, 512), BF),
            vmem((2, 8, 2, 16, 640), F32),
            vmem((2, 8, 16, 640), BF),
            vmem((2, 8, 16, 640), BF),
            vmem((2, 8, 16, 640), BF),
            vmem((2, 8, 16, 640), BF),
            vmem((16, 640), F32),
            dma(()),
            dma((NS,)),
            dma(()),
            dma((2, NS)),
            dma((2, NS)),
            dma((3,)),
            dma((2, NS)),
            dma((NS,)),
            dma((2,)),
            dma((2,)),
            dma((2,)),
            dma((2,)),
            dma((2,)),
            dma((2, 2)),
            dma((2, 2)),
            dma((14,)),
        ],
        compiler_params=pltpu.CompilerParams(
            collective_id=0, has_side_effects=True, vmem_limit_bytes=48 * 1000 * 1000
        ),
    )(
        *map(
            in_hbm,
            (
                resid,
                gain.reshape(1, 512),
                w_gate,
                w_up,
                w_down,
                cotangent,
                enc_tiles,
                enc_bias,
                dec_tiles,
                tile_blocks,
            ),
        ),
        owner_counts,
        in_hbm(token_blocks.T),
    )
    return resid_grad, attribution.transpose(1, 0, 2)


def solution(mesh):
    placed = (
        P(None, "tp"),
        P("tp"),
        P("tp", "lat"),
        P("tp", "lat"),
        P("lat", "tp"),
        P(None, "tp"),
        P("lat", "tp", None),
        P("lat", None),
        P("lat", None, "tp"),
        P("lat"),
        P("lat"),
        P(),
    )
    return jax.shard_map(
        on_device,
        mesh=mesh,
        in_specs=placed,
        out_specs=(P(None, "tp"), P("tp", "lat", None)),
        check_vma=False,
    )
```
